32 devices in a mesh: groups: 2 (over x), section: 2 (over core), tensor: 8 (over z, y).
Axes of the slice: x: 2, y: 2, z: 4, core: 2. Of those that a mesh axis runs over, the one named last changes fastest.
Arguments:
- hidden: bfloat16 [2, 1024, 26624], P('section', 'groups', 'tensor'), parts along dimension 1, may hold values from -6 to 6
- down_weight: bfloat16 [2, 26624, 8192], P('section', 'tensor'), may hold values from -0.0546875 to 0.0546875
- residual: bfloat16 [2, 1024, 8192], P('section', 'groups', 'tensor'), parts along dimension 1, may hold values from -100 to 100
- norm_gain: float32 [2, 8192], P('section'), may hold values from 0.1 to 1.9
- qkv_weight: bfloat16 [2, 8192, 9216], P('section', None, 'tensor'), may hold values from -0.0625 to 0.0625
Outputs:
- received: bfloat16 [2, 1024, 8192], P('section', 'groups', 'tensor'), parts along dimension 1
- projected: bfloat16 [2, 1024, 9216], P('section', 'groups', 'tensor'), parts along dimension 1
The draws below stay inside these ranges and needn't reach their ends.
There are 2 independent parts, one for each index of `groups`. The reference program is written for one: setup_inputs(seed, part) draws one part's arguments, and reference() takes and returns one part's arrays. A program takes and returns all parts, laid end to end along the dimension named above; an argument that names none is the same for every part. Nothing has to cross between parts.
All inputs are finite; a program needn't handle non-finite values.
Results may differ from the reference program's by a relative error of at most 0.0057.
Values may be sent and summed in bfloat16 or wider, within the bound.
No kernel may reach another device: no remote copies, remote signals or barrier semaphores. Data moves between devices by JAX's collectives and lax.ppermute only.
A program may use at most 192 MiB of HBM per device.

```python
import jax
import jax.numpy as jnp
from jax import lax

D = 8192
FF = 26624
TOK = 512
QKV = 9216
SECTIONS = 2


def draw_residual(key, part):
    key_base = jax.random.fold_in(key, 11)
    key_rows = jax.random.fold_in(key, 12)
    key_cols = jax.random.fold_in(key, 13)
    ramp = 10.0 ** (jnp.arange(D, dtype=jnp.float32) / D - 0.5)
    rough = jax.random.uniform(key_cols, (D,), jnp.float32, 0.5, 1.5)
    base = jax.random.truncated_normal(key_base, -6.0, 6.0, (SECTIONS, TOK, D), jnp.float32)
    rows = 10.0 ** jax.random.uniform(key_rows, (SECTIONS, TOK, 1), jnp.float32, -0.5, 0.5)
    return (base * rows * ramp[None, None, :] * rough[None, None, :]).astype(jnp.bfloat16)


def with_spikes(entries, rng, source, target, parts, factor):
    owner, partner = [(jnp.arange(entries.shape[dim]) // (entries.shape[dim] // parts)).reshape([-1 if axis == dim else 1 for axis in range(entries.ndim)]) for dim in (source, target)]
    chosen = jax.random.permutation(rng, parts)[partner]
    strong = (owner == chosen) | (owner == (partner + parts // 2) % parts)
    return jnp.where(strong, factor * entries, entries)


def levels(stream_key, extent, split, least, high):
    level, own = 1.0, jax.random.fold_in(stream_key, 6)
    for position, blocks in split:
        steps = jnp.exp(jax.random.uniform(jax.random.fold_in(own, position), (blocks,), jnp.float32, least / len(split), high / len(split)))
        level = level * jnp.repeat(steps, extent[position] // blocks).reshape([-1 if axis == position else 1 for axis in range(len(extent))])
    return level


def gaussian(key, extent, spread, reach, cuts=(), held_as=jnp.bfloat16):
    array = spread * jax.random.normal(key, extent, jnp.float32)
    if cuts:
        array = array * levels(key, extent, cuts, -0.22, 0.18)
    return jnp.clip(array, -reach, reach).astype(held_as)


def bell_draw_with(own_key, dims, deviation, bound, split, heavy, kind=jnp.bfloat16):
    array = deviation * jax.random.normal(own_key, dims, jnp.float32)
    if split:
        array = array * levels(own_key, dims, split, -0.22, 0.18)
    return jnp.clip(with_spikes(array, jax.random.fold_in(own_key, 3), *heavy), -bound, bound).astype(kind)


def setup_inputs(seed: int = 0, part: int = 0) -> dict:
    arg_keys = jax.random.split(jax.random.key(seed), 6)
    own_keys = jax.random.split(jax.random.fold_in(arg_keys[5], part), 6)
    return {
        "hidden": gaussian(own_keys[0], (SECTIONS, TOK, FF), 1.0, 6.0, ((0, 2), (2, 8))),
        "down_weight": bell_draw_with(arg_keys[1], (SECTIONS, FF, D), FF ** -0.5, 0.0546875, ((0, 2), (1, 8)), (1, 2, 8, 2.0)),
        "residual": draw_residual(jax.random.fold_in(jax.random.fold_in(arg_keys[5], part), 71), part),
        "norm_gain": jnp.clip(1.0 + 0.18 * jax.random.normal(arg_keys[3], (SECTIONS, D), jnp.float32), 0.1, 1.9),
        "qkv_weight": gaussian(arg_keys[4], (SECTIONS, D, QKV), D ** -0.5, 0.0625, ((0, 2), (2, 8))),
    }


epsilon = 1e-05

def reference(hidden, down_weight, residual, norm_gain, qkv_weight):
    streams = []
    for section_idx in range(SECTIONS):
        partial_sum = jnp.dot(hidden[section_idx], down_weight[section_idx], preferred_element_type=jnp.float32)
        streams.append((residual[section_idx].astype(jnp.float32) + partial_sum).astype(jnp.bfloat16))
    stream = jnp.stack(streams)
    received = jnp.roll(stream, 1, axis=0)
    outputs = []
    for section_idx in range(SECTIONS):
        floats = received[section_idx].astype(jnp.float32)
        square_sum = lax.optimization_barrier(jnp.sum(floats * floats, axis=1, keepdims=True))
        scale_inv = lax.rsqrt(square_sum / D + epsilon)
        normed = (floats * scale_inv * norm_gain[section_idx][None, :]).astype(jnp.bfloat16)
        outputs.append(jnp.dot(normed, qkv_weight[section_idx], preferred_element_type=jnp.float32).astype(jnp.bfloat16))
    return (received, jnp.stack(outputs))
```

```python
import jax
import jax.numpy as jnp
from jax import lax
from jax.sharding import PartitionSpec as P

epsilon = 1e-05
STREAMS = 4
RING_MAX = 8


def shifted(value, axis, steps):
    count = lax.axis_size(axis)
    pairs = [(source, (source + steps) % count) for source in range(count)]
    return lax.ppermute(value, axis, pairs)


def normalize(floats, gain_part):
    square_sum = jnp.sum(floats * floats, axis=1, keepdims=True)
    scale_inv = lax.rsqrt(square_sum / floats.shape[1] + epsilon)
    return (floats * scale_inv * gain_part[None, :]).astype(jnp.bfloat16)


def wide_body(hidden, down_weight, residual, norm_gain, qkv_weight):
    partial_sum = jnp.dot(hidden[0], down_weight[0], preferred_element_type=jnp.float32)
    summed = lax.psum_scatter(partial_sum, "tensor", scatter_dimension=1, tiled=True)
    stream = (residual[0].astype(jnp.float32) + summed).astype(jnp.bfloat16)
    received = shifted(stream, "section", 1)
    gathered = lax.all_gather(received, "tensor", axis=1, tiled=True)
    normed = normalize(gathered.astype(jnp.float32), norm_gain[0])
    projected = jnp.dot(normed, qkv_weight[0], preferred_element_type=jnp.float32).astype(jnp.bfloat16)
    return (received[None], projected[None])


def member(place, count):
    if isinstance(place, int):
        place = place % count
        return 2 * place if place < count // 2 else 2 * (count - 1 - place) + 1
    place = lax.rem(place + 2 * count, count)
    return jnp.where(place < count // 2, 2 * place, 2 * (count - 1 - place) + 1)


def ring_body(hidden, down_weight, residual, norm_gain, qkv_weight):
    count = lax.axis_size("tensor")
    sections = lax.axis_size("section")
    index = lax.axis_index("tensor")
    place = jnp.where(lax.rem(index, 2) == 0, index // 2, count - 1 - index // 2)
    hidden_local, down_local, residual_local = hidden[0], down_weight[0], residual[0]
    gain, qkv_local = norm_gain[0], qkv_weight[0]
    depth, features = down_local.shape
    share = features // count
    width = share // STREAMS
    ways = [1 if part < STREAMS // 2 else -1 for part in range(STREAMS)]
    order = [part for pair in zip(range(STREAMS // 2), range(STREAMS // 2, STREAMS)) for part in pair]
    hops = {way: [(member(p, count), member(p + way, count)) for p in range(count)] for way in (1, -1)}
    crossed = {
        way: [(s * count + a, (s + 1) % sections * count + b) for s in range(sections) for a, b in hops[way]]
        for way in (1, -1)
    }

    half = STREAMS // 2
    carried, sent = [None] * STREAMS, None
    for step in range(count):
        if sent is not None:
            hidden_local, _ = lax.optimization_barrier((hidden_local, sent))
        sums, sent = {}, []
        for way in (1, -1):
            column = member(place - way * (step + 1), count) * share + (0 if way > 0 else half * width)
            weights = lax.dynamic_slice(down_local, (0, column), (depth, half * width))
            sums[way] = jnp.dot(hidden_local, weights, preferred_element_type=jnp.float32)
        for part in order:
            total = sums[ways[part]][:, part % half * width : (part % half + 1) * width]
            if carried[part] is not None:
                total = total + carried[part].astype(jnp.float32)
            if step < count - 1:
                sent.append(total.astype(jnp.bfloat16))
                carried[part] = lax.ppermute(sent[-1], "tensor", hops[ways[part]])
            else:
                own = residual_local[:, part * width : (part + 1) * width].astype(jnp.float32)
                carried[part] = (own + total).astype(jnp.bfloat16)

    stream = carried
    held = [lax.ppermute(stream[part], ("section", "tensor"), crossed[ways[part]]) for part in range(STREAMS)]
    received = shifted(jnp.concatenate(stream, axis=1), "section", 1)

    def term(chunk, row):
        floats = chunk.astype(jnp.float32)
        rows = chunk.shape[1]
        scaled = (floats * lax.dynamic_slice(gain, (row,), (rows,))[None, :]).astype(jnp.bfloat16)
        weights = lax.dynamic_slice(qkv_local, (row, 0), (rows, qkv_local.shape[1]))
        return (
            jnp.dot(scaled, weights, preferred_element_type=jnp.float32),
            jnp.sum(floats * floats, axis=1, keepdims=True),
        )

    projected, squares = term(received, index * share)
    for step in range(1, count):
        for part in order:
            shard = member(place - ways[part] * step, count)
            product, square = term(held[part], shard * share + part * width)
            if step < count - 1:
                held[part] = lax.ppermute(held[part], "tensor", hops[ways[part]])
            projected, squares = projected + product, squares + square
    projected = (projected * lax.rsqrt(squares / features + epsilon)).astype(jnp.bfloat16)
    return (received[None], projected[None])


def solution(mesh):
    placed = (
        P("section", "groups", "tensor"),
        P("section", "tensor", None),
        P("section", "groups", "tensor"),
        P("section", None),
        P("section", None, "tensor"),
    )
    return jax.shard_map(
        ring_body if mesh.shape["tensor"] <= RING_MAX else wide_body,
        mesh=mesh,
        in_specs=placed,
        out_specs=(P("section", "groups", "tensor"), P("section", "groups", "tensor")),
        check_vma=False,
    )
```
